32 devices in a mesh: dp: 4 (over z), mp: 8 (over y, x, core).
Axes of the slice: x: 2, y: 2, z: 4, core: 2. Of those that a mesh axis runs over, the one named last changes fastest.
Arguments:
- tokens: bfloat16 [1024, 4096], P('dp', 'mp'), may hold values from -6 to 6
- weight_blocks: bfloat16 [2048, 4096], P('mp'), may hold values from -0.125 to 0.125
- block_rows: int32 [2048], P('mp'), may hold values from 0 to 63, as said below
- block_cols: int32 [2048], P('mp'), may hold values from 0 to 63, as said below
- importance: int32 [1024], P('dp'), may hold values from 1 to 64
- cotangent: bfloat16 [1024, 4096], P('dp', 'mp'), may hold values from -6 to 6
Outputs:
- projected: bfloat16 [1024, 4096], P('dp', 'mp')
- grad_input: bfloat16 [1024, 4096], P('dp', 'mp')
- grad_weight: bfloat16 [2048, 4096], P('mp')
The draws below stay inside these ranges and needn't reach their ends.
Inputs may be any that keep to these rules, and one draw needn't show every extreme that they name: `block_rows`: with block_cols, each (row block, column block) pair appears at most once. `block_cols`: of the 256 blocks of one device, those in its own column blocks come first, then the others by owning device; at most 3 lie in the column blocks of any one other device, and in every draw some device's column blocks have exactly 3 blocks on every other device.
All inputs are finite; a program needn't handle non-finite values.
Results may differ from the reference program's by a relative error of at most 0.017.
Values may be sent and summed in bfloat16 or wider, within the bound.
A program may use at most 128 MiB of HBM per device.

```python
import math
import jax
import jax.numpy as jnp
from jax import lax

D = 4096
BLOCK = 64
CB_DEV = 8
CAP = 3
TOK = 256
NRB = 64
FF = 4096
NB = 256
BLOCKS = 2048
TOKENS = 1024
N_DP = 4
N_MP = 8


def block_plan(seed_key):
    key_load, key_heavy, key_cells = jax.random.split(seed_key, 3)
    load_table = jnp.minimum(jnp.array([1, 1, 2, 2, 3, 3, 3, 3], dtype=jnp.int32), CAP)
    spill_counts = jnp.take(load_table, jax.random.randint(key_load, (N_MP, N_MP), 0, 8))
    heavy_owner = jax.random.randint(key_heavy, (), 0, N_MP)
    owners = jnp.arange(N_MP, dtype=jnp.int32)
    spill_counts = jnp.where(owners[None, :] == heavy_owner, CAP, spill_counts)
    spill_counts = jnp.where(owners[:, None] == owners[None, :], 0, spill_counts).astype(jnp.int32)
    home_counts = NB - jnp.sum(spill_counts, axis=1)
    cell_count = CB_DEV * NRB
    scores = jax.random.randint(key_cells, (N_MP, cell_count), 0, 1 << 20) * cell_count + jnp.arange(cell_count, dtype=jnp.int32)[None, :]
    cell_order = jnp.argsort(scores, axis=1).astype(jnp.int32)
    owner_start = home_counts[None, :] + jnp.cumsum(spill_counts, axis=0) - spill_counts
    holder_start = jnp.cumsum(spill_counts, axis=1) - spill_counts
    holder_end = holder_start + spill_counts
    entries = jnp.arange(NB, dtype=jnp.int32)
    spill_pos = entries[None, :] - home_counts[:, None]
    owner_of = jnp.sum((holder_end[:, None, :] <= spill_pos[:, :, None]).astype(jnp.int32), axis=2)
    owner_of = jnp.minimum(owner_of, N_MP - 1)
    list_start = jnp.take_along_axis(holder_start, owner_of, axis=1)
    owner_base = jnp.take_along_axis(owner_start, owner_of, axis=1)
    at_home = spill_pos < 0
    final_owner = jnp.where(at_home, owners[:, None], owner_of)
    position = jnp.where(at_home, entries[None, :], owner_base + spill_pos - list_start)
    cell_id = cell_order[final_owner, position]
    row_ids = (cell_id % NRB).astype(jnp.int32)
    col_ids = (final_owner * CB_DEV + cell_id // NRB).astype(jnp.int32)
    return (row_ids.reshape(-1), col_ids.reshape(-1))


def draw_block_rows(key, part):
    return block_plan(jax.random.fold_in(key, 11))[0]


def draw_block_cols(key, part):
    return block_plan(jax.random.fold_in(key, 11))[1]


def place_ends(values, own_key, low, top_value):
    longest = values.shape.index(max(values.shape))
    spots = []
    for shift in (0, 1):
        where = [jax.random.randint(jax.random.fold_in(own_key, axis), (), 0, length) for axis, length in enumerate(values.shape)]
        where[longest] = (where[longest] + shift) % values.shape[longest]
        spots.append(tuple(where))
    return values.at[spots[0]].set(low).at[spots[1]].set(top_value)


def block_levels(stream_key, extent, cuts, smallest, top_value):
    level = 1.0
    for dim, blocks in cuts:
        draws = jax.random.uniform(jax.random.fold_in(jax.random.fold_in(stream_key, 6), dim), (blocks,), jnp.float32, smallest / len(cuts), top_value / len(cuts))
        level = level * jnp.repeat(jnp.exp(draws), extent[dim] // blocks).reshape((-1,) + (1,) * (len(extent) - 1 - dim))
    return level


def centred(rng, dims, scale, reach, cuts=(), kind=jnp.bfloat16):
    values = scale * jax.random.normal(rng, dims, jnp.float32)
    if cuts:
        values = values * block_levels(rng, dims, cuts, -0.22, 0.18)
    return jnp.clip(values, -reach, reach).astype(kind)


def setup_inputs(seed: int = 0) -> dict:
    keys = jax.random.split(jax.random.key(seed), 7)
    return {
        "tokens": centred(keys[0], (TOKENS, D), 1.0, 6.0, ((0, 4), (1, 8))),
        "weight_blocks": centred(keys[1], (BLOCKS, BLOCK * BLOCK), (D // 2) ** -0.5, 0.125, ((0, 8),)),
        "block_rows": draw_block_rows(jax.random.fold_in(keys[6], 71), 0),
        "block_cols": draw_block_cols(jax.random.fold_in(keys[6], 71), 0),
        "importance": place_ends(jax.random.randint(keys[4], (TOKENS,), 1, 65), jax.random.fold_in(keys[4], 1), 1, 64).astype(jnp.int32),
        "cotangent": centred(keys[5], (TOKENS, FF), 1.0, 6.0, ((0, 4), (1, 8))),
    }


def reference(tokens, weight_blocks, block_rows, block_cols, importance, cotangent):
    col_total = CB_DEV * N_MP
    token_blocks = jnp.transpose(tokens).reshape(NRB, BLOCK, TOKENS)
    weighted = importance.astype(jnp.float32) / 64.0
    upstream = (jnp.transpose(cotangent).astype(jnp.float32) * weighted[None, :]).astype(jnp.bfloat16)
    grad_rows = upstream.reshape(col_total, BLOCK, TOKENS)
    grad_scale = 1.0 / math.sqrt(TOKENS)

    def per_holder(totals, pieces):
        out_sum, input_sum = totals
        holder, row_ids, col_ids, flat_weights = pieces
        blocks = flat_weights.reshape(NB, BLOCK, BLOCK).astype(jnp.float32)
        token_rows = jnp.take(token_blocks, row_ids, axis=0).astype(jnp.float32)
        partial_value = jnp.einsum('bkt,bkn->bnt', token_rows, blocks)
        rounded = lax.optimization_barrier(partial_value.astype(jnp.bfloat16)).astype(jnp.float32)
        spilled = col_ids // CB_DEV != holder
        partial_value = jnp.where(spilled[:, None, None], rounded, partial_value)
        out_sum = out_sum + jax.ops.segment_sum(partial_value, col_ids, num_segments=col_total)
        grad_blocks = jnp.take(grad_rows, col_ids, axis=0).astype(jnp.float32)
        input_terms = jnp.einsum('bnt,bkn->bkt', grad_blocks, blocks)
        input_sum = input_sum + jax.ops.segment_sum(input_terms, row_ids, num_segments=NRB)
        replica = jnp.einsum('bkgt,bngt->gbkn', token_rows.reshape(NB, BLOCK, N_DP, TOK), grad_blocks.reshape(NB, BLOCK, N_DP, TOK))
        replica = lax.optimization_barrier(replica.astype(jnp.bfloat16)).astype(jnp.float32)
        weight_grad = (lax.optimization_barrier(jnp.sum(replica, axis=0)) * grad_scale).astype(jnp.bfloat16)
        return ((out_sum, input_sum), weight_grad.reshape(NB, BLOCK * BLOCK))
    start_sums = (jnp.zeros((col_total, BLOCK, TOKENS), jnp.float32), jnp.zeros((NRB, BLOCK, TOKENS), jnp.float32))
    holders = jnp.arange(N_MP, dtype=jnp.int32)
    (out_sum, input_sum), grads_all = lax.scan(per_holder, start_sums, (holders, block_rows.reshape(N_MP, NB), block_cols.reshape(N_MP, NB), weight_blocks.reshape(N_MP, NB, BLOCK * BLOCK)))
    projected = jnp.transpose(out_sum.reshape(FF, TOKENS)).astype(jnp.bfloat16)
    grad_input = jnp.transpose(input_sum.reshape(D, TOKENS)).astype(jnp.bfloat16)
    return (projected, grad_input, grads_all.reshape(BLOCKS, BLOCK * BLOCK))
```

```python
import functools
import math

import jax
import jax.numpy as jnp
from jax import lax
from jax.experimental import pallas as pl
from jax.experimental.pallas import tpu as pltpu
from jax.sharding import PartitionSpec as P

BLOCK = 64
CAP = 3
GROUP = 8


def mm(a, b, dims=((1,), (0,))):
    return lax.dot_general(a, b, (dims, ((), ())), preferred_element_type=jnp.float32)


def swap_halves(x, y):
    width = x.shape[1]
    low = (lax.broadcasted_iota(jnp.int32, x.shape, 1) % 128) < 64
    first = jnp.where(low, x, pltpu.roll(y, 64, 1))
    second = jnp.where(low, pltpu.roll(x, width - 64, 1), y)
    return first, second


def dense_kernel(tok_ref, up_ref, w_ref, win_ref, crow_ref, crow_in_ref, ccol_ref, ccol_in_ref,
                 proj_ref, gi_ref, gw_ref, gw_in_ref,
                 wc_ref, wd_ref, gc_ref, gd_ref, acc_ref):
    d_count, tok_count, feat = tok_ref.shape
    cols = up_ref.shape[1]
    col_blocks = cols // BLOCK
    span = GROUP * BLOCK
    per = span // feat
    chunks = d_count // per
    cells = GROUP * col_blocks
    flat = BLOCK * BLOCK
    pairs = col_blocks // 2
    quads = BLOCK // 2
    src = lax.broadcasted_iota(jnp.int32, (span, span), 0)
    dst = lax.broadcasted_iota(jnp.int32, (span, span), 1)
    perm = ((src % BLOCK) * GROUP + src // BLOCK == dst).astype(jnp.float32).astype(jnp.bfloat16)
    acc_ref[...] = jnp.zeros_like(acc_ref)

    def chunk(j, _):
        base = j * cells
        ids = lax.broadcasted_iota(jnp.int32, (cells, 1), 0) + base
        hot = (ids == crow_ref[...]).astype(jnp.float32).astype(jnp.bfloat16)
        hot_in = (ids == crow_in_ref[...]).astype(jnp.float32).astype(jnp.bfloat16)
        wc_ref[...] = mm(hot, w_ref[...]) + mm(hot_in, win_ref[...])
        for p in range(pairs):
            a = wc_ref[2 * GROUP * p : 2 * GROUP * p + GROUP, :]
            b = wc_ref[2 * GROUP * p + GROUP : 2 * GROUP * (p + 1), :]
            even, odd = swap_halves(a, b)
            for q in range(quads):
                both = jnp.concatenate(
                    [even[:, 128 * q : 128 * (q + 1)], odd[:, 128 * q : 128 * (q + 1)]], axis=0
                )
                wd_ref[2 * GROUP * q : 2 * GROUP * (q + 1), 128 * p : 128 * (p + 1)] = both.astype(
                    jnp.bfloat16
                )
        parts = [tok_ref[j * per + g] for g in range(per)]
        tok = parts[0] if per == 1 else jnp.concatenate(parts, axis=1)
        tok_p = mm(tok, perm).astype(jnp.bfloat16)
        tok_t = mm(perm, tok, ((0,), (1,))).astype(jnp.bfloat16)
        acc_ref[...] += mm(tok_p, wd_ref[...])
        gi_p = mm(up_ref[...], wd_ref[...], ((1,), (1,))).astype(jnp.bfloat16)
        gi = mm(gi_p, perm, ((1,), (1,))).astype(jnp.bfloat16)
        for g in range(per):
            gi_ref[j * per + g] = gi[:, g * feat : (g + 1) * feat]
        gd_ref[...] = mm(tok_t, up_ref[...])
        for p in range(pairs):
            for q in range(quads):
                x = gd_ref[2 * GROUP * q : 2 * GROUP * q + GROUP, 128 * p : 128 * (p + 1)]
                y = gd_ref[2 * GROUP * q + GROUP : 2 * GROUP * (q + 1), 128 * p : 128 * (p + 1)]
                a, b = swap_halves(x, y)
                gc_ref[
                    pl.ds(pl.multiple_of(base + 2 * GROUP * p, 2 * GROUP), 2 * GROUP),
                    128 * q : 128 * (q + 1),
                ] = jnp.concatenate([a, b], axis=0).astype(jnp.bfloat16)
        return 0

    lax.fori_loop(0, chunks, chunk, 0)
    proj_ref[...] = acc_ref[...].astype(jnp.bfloat16)
    lanes = lax.broadcasted_iota(jnp.int32, (1, chunks * cells), 1)
    pick = (ccol_ref[...] == lanes).astype(jnp.float32).astype(jnp.bfloat16)
    pick_in = (ccol_in_ref[...] == lanes).astype(jnp.float32).astype(jnp.bfloat16)
    step = 512
    for s in range(flat // step):
        part = gc_ref[:, s * step : (s + 1) * step]
        gw_ref[:, s * step : (s + 1) * step] = mm(pick, part).astype(jnp.bfloat16)
        gw_in_ref[:, s * step : (s + 1) * step] = mm(pick_in, part).astype(jnp.bfloat16)


def dense_call(tok_all, up, weights, w_in, cell, cell_in):
    d_count, tok_count, feat = tok_all.shape
    cols = up.shape[1]
    span = GROUP * BLOCK
    cells = GROUP * (cols // BLOCK)
    chunks = d_count * feat // span
    flat = BLOCK * BLOCK
    nb, ns = weights.shape[0], w_in.shape[0]
    vm = pl.BlockSpec(memory_space=pltpu.VMEM)
    return pl.pallas_call(
        dense_kernel,
        out_shape=(
            jax.ShapeDtypeStruct((tok_count, cols), jnp.bfloat16),
            jax.ShapeDtypeStruct((d_count, tok_count, feat), jnp.bfloat16),
            jax.ShapeDtypeStruct((nb, flat), jnp.bfloat16),
            jax.ShapeDtypeStruct((ns, flat), jnp.bfloat16),
        ),
        in_specs=[vm] * 8,
        out_specs=(vm,) * 4,
        scratch_shapes=[
            pltpu.VMEM((cells, flat), jnp.float32),
            pltpu.VMEM((span, cols), jnp.bfloat16),
            pltpu.VMEM((chunks * cells, flat), jnp.bfloat16),
            pltpu.VMEM((span, cols), jnp.float32),
            pltpu.VMEM((tok_count, cols), jnp.float32),
        ],
        compiler_params=pltpu.CompilerParams(vmem_limit_bytes=48 * 1024 * 1024),
        name="dense",
    )(tok_all, up, weights, w_in, cell[None, :], cell_in[None, :], cell[:, None], cell_in[:, None])


def cell_of(row, col):
    return (row // GROUP) * (GROUP * GROUP) + col * GROUP + row % GROUP


def plan(block_rows, block_cols, col_blocks, model_count, my_index):
    nb = block_rows.shape[0]
    target = block_cols // col_blocks
    home = target == my_index
    entry = jnp.arange(nb)
    earlier = (entry[None, :] < entry[:, None]) & (target[None, :] == target[:, None])
    rank = jnp.sum(earlier.astype(jnp.int32), axis=1)
    slot = jnp.where(home, -1, target * CAP + rank)
    local_col = block_cols % col_blocks
    return home, slot, local_col


def per_device(tokens, weight_blocks, block_rows, block_cols, importance, cotangent):
    tok_count = tokens.shape[0]
    model_count = lax.axis_size("mp")
    data_count = lax.axis_size("dp")
    my_index = lax.axis_index("mp")
    col_blocks = cotangent.shape[1] // BLOCK
    slots = model_count * CAP
    flat = BLOCK * BLOCK
    grad_scale = 1.0 / math.sqrt(tok_count * data_count)
    gathered = lax.all_gather(tokens, "mp", axis=0)
    home, slot, local_col = plan(block_rows, block_cols, col_blocks, model_count, my_index)
    send_hot = (jnp.arange(slots)[:, None] == slot[None, :])
    hot16 = send_hot.astype(jnp.bfloat16)
    payload = jnp.dot(hot16, weight_blocks, preferred_element_type=jnp.float32).astype(jnp.bfloat16)
    used = jnp.sum(send_hot * (local_col + 1)[None, :], axis=1)
    rows = jnp.sum(send_hot * block_rows[None, :], axis=1)
    meta = jnp.stack([rows, used], axis=1).astype(jnp.bfloat16)
    meta = jnp.pad(meta, ((0, 0), (0, 126)))
    payload = jnp.concatenate([payload, meta], axis=1).reshape(model_count, CAP, flat + 128)
    arrived = lax.all_to_all(payload, "mp", split_axis=0, concat_axis=0, tiled=True)
    arrived = arrived.reshape(slots, flat + 128)
    w_in = arrived[:, :flat]
    row_in = arrived[:, flat].astype(jnp.int32)
    col_in = arrived[:, flat + 1].astype(jnp.int32) - 1
    cell = jnp.where(home, cell_of(block_rows, local_col), -1)
    cell_in = jnp.where(col_in >= 0, cell_of(row_in, col_in), -1)
    weighted = importance.astype(jnp.float32) / 64.0
    up = (cotangent.astype(jnp.float32) * weighted[:, None]).astype(jnp.bfloat16)
    projected, gi_parts, gw, gw_in = dense_call(gathered, up, weight_blocks, w_in, cell, cell_in)
    returned = lax.all_to_all(
        gw_in.reshape(model_count, CAP, flat), "mp", split_axis=0, concat_axis=0, tiled=True
    ).reshape(slots, flat)
    back = lax.dot_general(
        hot16, returned, (((0,), (0,)), ((), ())), preferred_element_type=jnp.float32
    ).astype(jnp.bfloat16)
    gw = jnp.where(home[:, None], gw, back)
    weight_sum = lax.psum(gw, "dp").astype(jnp.float32)
    grad_weight = (weight_sum * grad_scale).astype(jnp.bfloat16)
    grad_input = lax.psum_scatter(gi_parts, "mp", scatter_dimension=0, tiled=False)
    return (projected, grad_input, grad_weight)


def solution(mesh):
    return jax.shard_map(
        per_device,
        mesh=mesh,
        in_specs=(P("dp", "mp"), P("mp", None), P("mp"), P("mp"), P("dp"), P("dp", "mp")),
        out_specs=(P("dp", "mp"), P("dp", "mp"), P("mp", None)),
        check_vma=False,
    )
```

```python
import functools
import math

import jax
import jax.numpy as jnp
from jax import lax
from jax.experimental import pallas as pl
from jax.experimental.pallas import tpu as pltpu
from jax.sharding import PartitionSpec as P

BLOCK = 64
CAP = 3
GROUP = 8


def mm(a, b, dims=((1,), (0,))):
    return lax.dot_general(a, b, (dims, ((), ())), preferred_element_type=jnp.float32)


def swap_halves(x, y):
    width = x.shape[1]
    low = (lax.broadcasted_iota(jnp.int32, x.shape, 1) % 128) < 64
    first = jnp.where(low, x, pltpu.roll(y, 64, 1))
    second = jnp.where(low, pltpu.roll(x, width - 64, 1), y)
    return first, second


def dense_kernel(tok_ref, up_ref, w_ref, win_ref, crow_ref, crow_in_ref, ccol_ref, ccol_in_ref,
                 proj_ref, gi_ref, gw_ref, gw_in_ref,
                 wc_ref, wd_ref, gc_ref, gd_ref, acc_ref):
    d_count, tok_count, feat = tok_ref.shape
    cols = up_ref.shape[1]
    col_blocks = cols // BLOCK
    span = GROUP * BLOCK
    per = span // feat
    chunks = d_count // per
    cells = GROUP * col_blocks
    flat = BLOCK * BLOCK
    pairs = col_blocks // 2
    quads = BLOCK // 2
    src = lax.broadcasted_iota(jnp.int32, (span, span), 0)
    dst = lax.broadcasted_iota(jnp.int32, (span, span), 1)
    perm = ((src % BLOCK) * GROUP + src // BLOCK == dst).astype(jnp.float32).astype(jnp.bfloat16)
    acc_ref[...] = jnp.zeros_like(acc_ref)

    def chunk(j, _):
        base = j * cells
        ids = lax.broadcasted_iota(jnp.int32, (cells, 1), 0) + base
        hot = (ids == crow_ref[...]).astype(jnp.float32).astype(jnp.bfloat16)
        hot_in = (ids == crow_in_ref[...]).astype(jnp.float32).astype(jnp.bfloat16)
        wc_ref[...] = mm(hot, w_ref[...]) + mm(hot_in, win_ref[...])
        for p in range(pairs):
            a = wc_ref[2 * GROUP * p : 2 * GROUP * p + GROUP, :]
            b = wc_ref[2 * GROUP * p + GROUP : 2 * GROUP * (p + 1), :]
            even, odd = swap_halves(a, b)
            for q in range(quads):
                both = jnp.concatenate(
                    [even[:, 128 * q : 128 * (q + 1)], odd[:, 128 * q : 128 * (q + 1)]], axis=0
                )
                wd_ref[2 * GROUP * q : 2 * GROUP * (q + 1), 128 * p : 128 * (p + 1)] = both.astype(
                    jnp.bfloat16
                )
        parts = [tok_ref[j * per + g] for g in range(per)]
        tok = parts[0] if per == 1 else jnp.concatenate(parts, axis=1)
        tok_p = mm(tok, perm).astype(jnp.bfloat16)
        tok_t = mm(perm, tok, ((0,), (1,))).astype(jnp.bfloat16)
        acc_ref[...] += mm(tok_p, wd_ref[...])
        gi_p = mm(up_ref[...], wd_ref[...], ((1,), (1,))).astype(jnp.bfloat16)
        gi = mm(gi_p, perm, ((1,), (1,))).astype(jnp.bfloat16)
        for g in range(per):
            gi_ref[j * per + g] = gi[:, g * feat : (g + 1) * feat]
        gd_ref[...] = mm(tok_t, up_ref[...])
        for p in range(pairs):
            for q in range(quads):
                x = gd_ref[2 * GROUP * q : 2 * GROUP * q + GROUP, 128 * p : 128 * (p + 1)]
                y = gd_ref[2 * GROUP * q + GROUP : 2 * GROUP * (q + 1), 128 * p : 128 * (p + 1)]
                a, b = swap_halves(x, y)
                gc_ref[
                    pl.ds(pl.multiple_of(base + 2 * GROUP * p, 2 * GROUP), 2 * GROUP),
                    128 * q : 128 * (q + 1),
                ] = jnp.concatenate([a, b], axis=0).astype(jnp.bfloat16)
        return 0

    lax.fori_loop(0, chunks, chunk, 0)
    proj_ref[...] = acc_ref[...].astype(jnp.bfloat16)
    lanes = lax.broadcasted_iota(jnp.int32, (1, chunks * cells), 1)
    pick = (ccol_ref[...] == lanes).astype(jnp.float32).astype(jnp.bfloat16)
    pick_in = (ccol_in_ref[...] == lanes).astype(jnp.float32).astype(jnp.bfloat16)
    step = 512
    for s in range(flat // step):
        part = gc_ref[:, s * step : (s + 1) * step]
        gw_ref[:, s * step : (s + 1) * step] = mm(pick, part).astype(jnp.bfloat16)
        gw_in_ref[:, s * step : (s + 1) * step] = mm(pick_in, part).astype(jnp.bfloat16)


def dense_call(tok_all, up, weights, w_in, cell, cell_in):
    d_count, tok_count, feat = tok_all.shape
    cols = up.shape[1]
    span = GROUP * BLOCK
    cells = GROUP * (cols // BLOCK)
    chunks = d_count * feat // span
    flat = BLOCK * BLOCK
    nb, ns = weights.shape[0], w_in.shape[0]
    vm = pl.BlockSpec(memory_space=pltpu.VMEM)
    return pl.pallas_call(
        dense_kernel,
        out_shape=(
            jax.ShapeDtypeStruct((tok_count, cols), jnp.bfloat16),
            jax.ShapeDtypeStruct((d_count, tok_count, feat), jnp.bfloat16),
            jax.ShapeDtypeStruct((nb, flat), jnp.bfloat16),
            jax.ShapeDtypeStruct((ns, flat), jnp.bfloat16),
        ),
        in_specs=[vm] * 8,
        out_specs=(vm,) * 4,
        scratch_shapes=[
            pltpu.VMEM((cells, flat), jnp.float32),
            pltpu.VMEM((span, cols), jnp.bfloat16),
            pltpu.VMEM((chunks * cells, flat), jnp.bfloat16),
            pltpu.VMEM((span, cols), jnp.float32),
            pltpu.VMEM((tok_count, cols), jnp.float32),
        ],
        compiler_params=pltpu.CompilerParams(vmem_limit_bytes=48 * 1024 * 1024),
        name="dense",
    )(tok_all, up, weights, w_in, cell[None, :], cell_in[None, :], cell[:, None], cell_in[:, None])


MESH = pl.DeviceIdType.MESH
ROWS = 16


def reduce_kernel(scale, gw_ref, gi_ref, gin_ref, hot_ref, gw_out, gi_out,
                  rbuf, sbuf, gbuf, ret, flatret, tail, tot,
                  r_send, r_recv, b_send, b_recv, g_send, g_recv, q_send, q_recv):
    me, z = lax.axis_index("mp"), lax.axis_index("dp")
    n_mp, n = lax.axis_size("mp"), lax.axis_size("dp")
    nb, flat = gw_ref.shape
    half = flat // 2
    count = nb // ROWS
    tail_rows = tail.shape[0]
    cap = gin_ref.shape[1]
    first_tail = count - tail_rows // ROWS
    low, high = z > 0, z < n - 1

    barrier = pltpu.get_barrier_semaphore()

    def peer(i):
        return lax.rem(me + i, n_mp)

    def greet(i, _):
        pl.semaphore_signal(barrier, inc=1, device_id={"mp": peer(i)}, device_id_type=MESH)
        return 0

    lax.fori_loop(1, n_mp, greet, 0)

    @pl.when(low)
    def _():
        pl.semaphore_signal(barrier, inc=1, device_id={"dp": z - 1}, device_id_type=MESH)

    @pl.when(high)
    def _():
        pl.semaphore_signal(barrier, inc=1, device_id={"dp": z + 1}, device_id_type=MESH)

    pl.semaphore_wait(barrier, n_mp - 1 + low.astype(jnp.int32) + high.astype(jnp.int32))

    def back_copy(i, into):
        d = peer(i)
        return pltpu.make_async_remote_copy(
            src_ref=gin_ref.at[d], dst_ref=ret.at[me if into is None else into],
            send_sem=q_send.at[d], recv_sem=q_recv.at[me if into is None else into],
            device_id={"mp": d}, device_id_type=MESH)

    def gi_copy(i, into):
        d = peer(i)
        return pltpu.make_async_remote_copy(
            src_ref=gi_ref.at[d], dst_ref=gbuf.at[me if into is None else into],
            send_sem=g_send.at[d], recv_sem=g_recv.at[me if into is None else into],
            device_id={"mp": d}, device_id_type=MESH)

    def start_back(i, _):
        back_copy(i, None).start()
        return 0

    def start_gi(i, _):
        gi_copy(i, None).start()
        return 0

    lax.fori_loop(1, n_mp, start_back, 0)
    lax.fori_loop(1, n_mp, start_gi, 0)
    ret[me] = jnp.zeros(ret.shape[1:], ret.dtype)

    def rows_of(c):
        return pl.ds(pl.multiple_of(c * ROWS, ROWS), ROWS)

    def lanes_of(h):
        return slice(h * half, (h + 1) * half)

    def chain(h, side, c):
        target = z + 1 if side == 0 else z - 1
        return pltpu.make_async_remote_copy(
            src_ref=sbuf.at[h, rows_of(c)], dst_ref=rbuf.at[h, side, rows_of(c)],
            send_sem=r_send.at[h, c], recv_sem=r_recv.at[h, side, c],
            device_id={"dp": target}, device_id_type=MESH)

    def spread(h, side, c):
        target = z + 1 if side == 0 else z - 1
        return pltpu.make_async_remote_copy(
            src_ref=gw_out.at[rows_of(c), lanes_of(h)], dst_ref=gw_out.at[rows_of(c), lanes_of(h)],
            send_sem=b_send.at[h, side, c], recv_sem=b_recv.at[h, c],
            device_id={"dp": target}, device_id_type=MESH)

    def send_out(h, c, root):
        @pl.when(low & (z <= root))
        def _():
            spread(h, 1, c).start()

        @pl.when(high & (z >= root))
        def _():
            spread(h, 0, c).start()

    def gather_in(own_ref, offset, c):
        for h in range(2):
            root = n // 2 - h
            tot[...] = own_ref[rows_of(c - offset), lanes_of(h)].astype(jnp.float32)

            @pl.when(low & (z <= root))
            def _():
                chain(h, 0, c).wait_recv()
                tot[...] += rbuf[h, 0, rows_of(c)].astype(jnp.float32)

            @pl.when(high & (z >= root))
            def _():
                chain(h, 1, c).wait_recv()
                tot[...] += rbuf[h, 1, rows_of(c)].astype(jnp.float32)

            @pl.when(z == root)
            def _():
                gw_out[rows_of(c), lanes_of(h)] = (tot[...] * scale).astype(jnp.bfloat16)
                send_out(h, c, root)

            @pl.when(z != root)
            def _():
                sbuf[h, rows_of(c)] = tot[...].astype(jnp.bfloat16)

            @pl.when(z < root)
            def _():
                chain(h, 0, c).start()

            @pl.when(z > root)
            def _():
                chain(h, 1, c).start()

    def pass_out(c):
        for h in range(2):
            root = n // 2 - h

            @pl.when(z != root)
            def _():
                spread(h, 0, c).wait_recv()
                send_out(h, c, root)

    lag = n

    def body(own_ref, offset):
        def step(s, _):
            gather_in(own_ref, offset, s)

            @pl.when(s >= lag)
            def _():
                pass_out(s - lag)

            return 0

        return step

    lax.fori_loop(0, first_tail, body(gw_ref, 0), 0)

    def wait_back(i, _):
        back_copy(i, peer(i)).wait_recv()
        return 0

    lax.fori_loop(1, n_mp, wait_back, 0)
    for d in range(n_mp):
        flatret[d * cap : (d + 1) * cap, :] = ret[d].astype(jnp.float32)
    start = first_tail * ROWS
    tail[...] = (
        gw_ref[start:nb, :].astype(jnp.float32)
        + mm(hot_ref[...], flatret[...].astype(jnp.bfloat16))
    ).astype(jnp.bfloat16)
    lax.fori_loop(first_tail, count, body(tail, first_tail), 0)

    def drain(s, _):
        pass_out(s)
        return 0

    lax.fori_loop(max(count - lag, 0), count, drain, 0)

    def finish(i, _):
        gi_copy(i, peer(i)).wait_recv()
        return 0

    lax.fori_loop(1, n_mp, finish, 0)
    total = gi_ref[me].astype(jnp.float32)
    gbuf[me] = jnp.zeros(gbuf.shape[1:], gbuf.dtype)
    for d in range(n_mp):
        total = total + gbuf[d].astype(jnp.float32)
    gi_out[...] = total.astype(jnp.bfloat16)

    def sent(i, _):
        back_copy(i, None).wait_send()
        gi_copy(i, None).wait_send()
        return 0

    lax.fori_loop(1, n_mp, sent, 0)

    def sent_z(c, _):
        for h in range(2):
            root = n // 2 - h

            @pl.when(z != root)
            def _():
                chain(h, 0, c).wait_send()

            @pl.when(low & (z <= root))
            def _():
                spread(h, 1, c).wait_send()

            @pl.when(high & (z >= root))
            def _():
                spread(h, 0, c).wait_send()

        return 0

    lax.fori_loop(0, count, sent_z, 0)


def reduce_call(gw, gi_parts, gw_in, hot_tail, scale, data_count):
    nb, flat = gw.shape
    n_mp, tok_count, feat = gi_parts.shape
    count, half = nb // ROWS, flat // 2
    cap = gw_in.shape[1]
    dma = pltpu.SemaphoreType.DMA
    vm = pl.BlockSpec(memory_space=pltpu.VMEM)
    return pl.pallas_call(
        functools.partial(reduce_kernel, scale),
        out_shape=(
            jax.ShapeDtypeStruct((nb, flat), jnp.bfloat16),
            jax.ShapeDtypeStruct((tok_count, feat), jnp.bfloat16),
        ),
        in_specs=[vm] * 4,
        out_specs=(vm,) * 2,
        scratch_shapes=[
            pltpu.VMEM((2, 2, nb, half), jnp.bfloat16),
            pltpu.VMEM((2, nb, half), jnp.bfloat16),
            pltpu.VMEM(gi_parts.shape, jnp.bfloat16),
            pltpu.VMEM(gw_in.shape, jnp.bfloat16),
            pltpu.VMEM((n_mp * cap, flat), jnp.float32),
            pltpu.VMEM((hot_tail.shape[0], flat), jnp.bfloat16),
            pltpu.VMEM((ROWS, half), jnp.float32),
            dma((2, count)), dma((2, 2, count)), dma((2, 2, count)), dma((2, count)),
            dma((n_mp,)), dma((n_mp,)), dma((n_mp,)), dma((n_mp,)),
        ],
        compiler_params=pltpu.CompilerParams(
            collective_id=0, has_side_effects=True, vmem_limit_bytes=48 * 1024 * 1024
        ),
        name="reduce",
    )(gw, gi_parts, gw_in, hot_tail)


def cell_of(row, col):
    return (row // GROUP) * (GROUP * GROUP) + col * GROUP + row % GROUP


def plan(block_rows, block_cols, col_blocks, model_count, my_index):
    nb = block_rows.shape[0]
    target = block_cols // col_blocks
    home = target == my_index
    entry = jnp.arange(nb)
    earlier = (entry[None, :] < entry[:, None]) & (target[None, :] == target[:, None])
    rank = jnp.sum(earlier.astype(jnp.int32), axis=1)
    slot = jnp.where(home, -1, target * CAP + rank)
    local_col = block_cols % col_blocks
    return home, slot, local_col


def per_device(tokens, weight_blocks, block_rows, block_cols, importance, cotangent):
    tok_count = tokens.shape[0]
    model_count = lax.axis_size("mp")
    data_count = lax.axis_size("dp")
    my_index = lax.axis_index("mp")
    col_blocks = cotangent.shape[1] // BLOCK
    slots = model_count * CAP
    flat = BLOCK * BLOCK
    grad_scale = 1.0 / math.sqrt(tok_count * data_count)
    gathered = lax.all_gather(tokens, "mp", axis=0)
    home, slot, local_col = plan(block_rows, block_cols, col_blocks, model_count, my_index)
    send_hot = (jnp.arange(slots)[:, None] == slot[None, :])
    hot16 = send_hot.astype(jnp.bfloat16)
    payload = jnp.dot(hot16, weight_blocks, preferred_element_type=jnp.float32).astype(jnp.bfloat16)
    used = jnp.sum(send_hot * (local_col + 1)[None, :], axis=1)
    rows = jnp.sum(send_hot * block_rows[None, :], axis=1)
    meta = jnp.stack([rows, used], axis=1).astype(jnp.bfloat16)
    meta = jnp.pad(meta, ((0, 0), (0, 126)))
    payload = jnp.concatenate([payload, meta], axis=1).reshape(model_count, CAP, flat + 128)
    arrived = lax.all_to_all(payload, "mp", split_axis=0, concat_axis=0, tiled=True)
    arrived = arrived.reshape(slots, flat + 128)
    w_in = arrived[:, :flat]
    row_in = arrived[:, flat].astype(jnp.int32)
    col_in = arrived[:, flat + 1].astype(jnp.int32) - 1
    cell = jnp.where(home, cell_of(block_rows, local_col), -1)
    cell_in = jnp.where(col_in >= 0, cell_of(row_in, col_in), -1)
    weighted = importance.astype(jnp.float32) / 64.0
    up = (cotangent.astype(jnp.float32) * weighted[:, None]).astype(jnp.bfloat16)
    projected, gi_parts, gw, gw_in = dense_call(gathered, up, weight_blocks, w_in, cell, cell_in)
    tail_rows = min(-(-slots // ROWS) * ROWS, block_rows.shape[0])
    hot_tail = hot16.T[block_rows.shape[0] - tail_rows :]
    grad_weight, grad_input = reduce_call(
        gw, gi_parts, gw_in.reshape(model_count, CAP, flat), hot_tail, grad_scale, data_count
    )
    return (projected, grad_input, grad_weight)


def solution(mesh):
    return jax.shard_map(
        per_device,
        mesh=mesh,
        in_specs=(P("dp", "mp"), P("mp", None), P("mp"), P("mp"), P("dp"), P("dp", "mp")),
        out_specs=(P("dp", "mp"), P("dp", "mp"), P("mp", None)),
        check_vma=False,
    )
```

```python
import functools
import math

import jax
import jax.numpy as jnp
from jax import lax
from jax.experimental import pallas as pl
from jax.experimental.pallas import tpu as pltpu
from jax.sharding import PartitionSpec as P

BLOCK = 64
CAP = 3
GROUP = 8


def mm(a, b, dims=((1,), (0,))):
    return lax.dot_general(a, b, (dims, ((), ())), preferred_element_type=jnp.float32)


def swap_halves(x, y):
    width = x.shape[1]
    low = (lax.broadcasted_iota(jnp.int32, x.shape, 1) % 128) < 64
    first = jnp.where(low, x, pltpu.roll(y, 64, 1))
    second = jnp.where(low, pltpu.roll(x, width - 64, 1), y)
    return first, second


def dense_kernel(tok_ref, up_ref, w_ref, win_ref, crow_ref, crow_in_ref, ccol_ref, ccol_in_ref,
                 proj_ref, gi_ref, gw_ref, gw_in_ref,
                 wc_ref, wd_ref, gc_ref, gd_ref, acc_ref):
    d_count, tok_count, feat = tok_ref.shape
    cols = up_ref.shape[1]
    col_blocks = cols // BLOCK
    span = GROUP * BLOCK
    per = span // feat
    chunks = d_count // per
    cells = GROUP * col_blocks
    flat = BLOCK * BLOCK
    pairs = col_blocks // 2
    quads = BLOCK // 2
    src = lax.broadcasted_iota(jnp.int32, (span, span), 0)
    dst = lax.broadcasted_iota(jnp.int32, (span, span), 1)
    perm = ((src % BLOCK) * GROUP + src // BLOCK == dst).astype(jnp.float32).astype(jnp.bfloat16)
    acc_ref[...] = jnp.zeros_like(acc_ref)

    def chunk(j, _):
        base = j * cells
        ids = lax.broadcasted_iota(jnp.int32, (cells, 1), 0) + base
        hot = (ids == crow_ref[...]).astype(jnp.float32).astype(jnp.bfloat16)
        hot_in = (ids == crow_in_ref[...]).astype(jnp.float32).astype(jnp.bfloat16)
        wc_ref[...] = mm(hot, w_ref[...]) + mm(hot_in, win_ref[...])
        for p in range(pairs):
            a = wc_ref[2 * GROUP * p : 2 * GROUP * p + GROUP, :]
            b = wc_ref[2 * GROUP * p + GROUP : 2 * GROUP * (p + 1), :]
            even, odd = swap_halves(a, b)
            for q in range(quads):
                both = jnp.concatenate(
                    [even[:, 128 * q : 128 * (q + 1)], odd[:, 128 * q : 128 * (q + 1)]], axis=0
                )
                wd_ref[2 * GROUP * q : 2 * GROUP * (q + 1), 128 * p : 128 * (p + 1)] = both.astype(
                    jnp.bfloat16
                )
        parts = [tok_ref[j * per + g] for g in range(per)]
        tok = parts[0] if per == 1 else jnp.concatenate(parts, axis=1)
        tok_p = mm(tok, perm).astype(jnp.bfloat16)
        tok_t = mm(perm, tok, ((0,), (1,))).astype(jnp.bfloat16)
        acc_ref[...] += mm(tok_p, wd_ref[...])
        gi_p = mm(up_ref[...], wd_ref[...], ((1,), (1,))).astype(jnp.bfloat16)
        gi = mm(gi_p, perm, ((1,), (1,))).astype(jnp.bfloat16)
        for g in range(per):
            gi_ref[j * per + g] = gi[:, g * feat : (g + 1) * feat]
        gd_ref[...] = mm(tok_t, up_ref[...])
        for p in range(pairs):
            for q in range(quads):
                x = gd_ref[2 * GROUP * q : 2 * GROUP * q + GROUP, 128 * p : 128 * (p + 1)]
                y = gd_ref[2 * GROUP * q + GROUP : 2 * GROUP * (q + 1), 128 * p : 128 * (p + 1)]
                a, b = swap_halves(x, y)
                gc_ref[
                    pl.ds(pl.multiple_of(base + 2 * GROUP * p, 2 * GROUP), 2 * GROUP),
                    128 * q : 128 * (q + 1),
                ] = jnp.concatenate([a, b], axis=0).astype(jnp.bfloat16)
        return 0

    lax.fori_loop(0, chunks, chunk, 0)
    proj_ref[...] = acc_ref[...].astype(jnp.bfloat16)
    lanes = lax.broadcasted_iota(jnp.int32, (1, chunks * cells), 1)
    pick = (ccol_ref[...] == lanes).astype(jnp.float32).astype(jnp.bfloat16)
    pick_in = (ccol_in_ref[...] == lanes).astype(jnp.float32).astype(jnp.bfloat16)
    step = 512
    for s in range(flat // step):
        part = gc_ref[:, s * step : (s + 1) * step]
        gw_ref[:, s * step : (s + 1) * step] = mm(pick, part).astype(jnp.bfloat16)
        gw_in_ref[:, s * step : (s + 1) * step] = mm(pick_in, part).astype(jnp.bfloat16)


def dense_call(tok_all, up, weights, w_in, cell, cell_in):
    d_count, tok_count, feat = tok_all.shape
    cols = up.shape[1]
    span = GROUP * BLOCK
    cells = GROUP * (cols // BLOCK)
    chunks = d_count * feat // span
    flat = BLOCK * BLOCK
    nb, ns = weights.shape[0], w_in.shape[0]
    vm = pl.BlockSpec(memory_space=pltpu.VMEM)
    return pl.pallas_call(
        dense_kernel,
        out_shape=(
            jax.ShapeDtypeStruct((tok_count, cols), jnp.bfloat16),
            jax.ShapeDtypeStruct((d_count, tok_count, feat), jnp.bfloat16),
            jax.ShapeDtypeStruct((nb, flat), jnp.bfloat16),
            jax.ShapeDtypeStruct((ns, flat), jnp.bfloat16),
        ),
        in_specs=[vm] * 8,
        out_specs=(vm,) * 4,
        scratch_shapes=[
            pltpu.VMEM((cells, flat), jnp.float32),
            pltpu.VMEM((span, cols), jnp.bfloat16),
            pltpu.VMEM((chunks * cells, flat), jnp.bfloat16),
            pltpu.VMEM((span, cols), jnp.float32),
            pltpu.VMEM((tok_count, cols), jnp.float32),
        ],
        compiler_params=pltpu.CompilerParams(vmem_limit_bytes=48 * 1024 * 1024),
        name="dense",
    )(tok_all, up, weights, w_in, cell[None, :], cell_in[None, :], cell[:, None], cell_in[:, None])


MESH = pl.DeviceIdType.MESH
ROWS = 16
SLACK = 2


def reduce_kernel(scale, gw_ref, gi_ref, gin_ref, hot_ref, gw_out, gi_out,
                  rbuf, sbuf, gbuf, ret, flatret, tail, tot,
                  r_send, r_recv, b_send, b_recv, g_send, g_recv, q_send, q_recv):
    me, z = lax.axis_index("mp"), lax.axis_index("dp")
    n_mp, n = lax.axis_size("mp"), lax.axis_size("dp")
    nb, flat = gw_ref.shape
    half = flat // 2
    count = nb // ROWS
    tail_rows = tail.shape[0]
    cap = gin_ref.shape[1]
    first_tail = count - tail_rows // ROWS
    low, high = z > 0, z < n - 1

    barrier = pltpu.get_barrier_semaphore()

    def peer(i):
        return lax.rem(me + i, n_mp)

    def greet(i, _):
        pl.semaphore_signal(barrier, inc=1, device_id={"mp": peer(i)}, device_id_type=MESH)
        return 0

    lax.fori_loop(1, n_mp, greet, 0)

    @pl.when(low)
    def _():
        pl.semaphore_signal(barrier, inc=1, device_id={"dp": z - 1}, device_id_type=MESH)

    @pl.when(high)
    def _():
        pl.semaphore_signal(barrier, inc=1, device_id={"dp": z + 1}, device_id_type=MESH)

    pl.semaphore_wait(barrier, n_mp - 1 + low.astype(jnp.int32) + high.astype(jnp.int32))

    def back_copy(i, into):
        d = peer(i)
        return pltpu.make_async_remote_copy(
            src_ref=gin_ref.at[d], dst_ref=ret.at[me if into is None else into],
            send_sem=q_send.at[d], recv_sem=q_recv.at[me if into is None else into],
            device_id={"mp": d}, device_id_type=MESH)

    def gi_copy(i, into):
        d = peer(i)
        return pltpu.make_async_remote_copy(
            src_ref=gi_ref.at[d], dst_ref=gbuf.at[me if into is None else into],
            send_sem=g_send.at[d], recv_sem=g_recv.at[me if into is None else into],
            device_id={"mp": d}, device_id_type=MESH)

    def start_back(i, _):
        back_copy(i, None).start()
        return 0

    def start_gi(i, _):
        gi_copy(i, None).start()
        return 0

    lax.fori_loop(1, n_mp, start_back, 0)
    lax.fori_loop(1, n_mp, start_gi, 0)
    ret[me] = jnp.zeros(ret.shape[1:], ret.dtype)

    def rows_of(c):
        return pl.ds(pl.multiple_of(c * ROWS, ROWS), ROWS)

    def lanes_of(h):
        return slice(h * half, (h + 1) * half)

    def chain(h, side, c):
        target = z + 1 if side == 0 else z - 1
        return pltpu.make_async_remote_copy(
            src_ref=sbuf.at[h, rows_of(c)], dst_ref=rbuf.at[h, side, rows_of(c)],
            send_sem=r_send.at[h, c], recv_sem=r_recv.at[h, side, c],
            device_id={"dp": target}, device_id_type=MESH)

    def spread(h, side, c):
        target = z + 1 if side == 0 else z - 1
        return pltpu.make_async_remote_copy(
            src_ref=gw_out.at[rows_of(c), lanes_of(h)], dst_ref=gw_out.at[rows_of(c), lanes_of(h)],
            send_sem=b_send.at[h, side, c], recv_sem=b_recv.at[h, c],
            device_id={"dp": target}, device_id_type=MESH)

    def send_out(h, c, root):
        @pl.when(low & (z <= root))
        def _():
            spread(h, 1, c).start()

        @pl.when(high & (z >= root))
        def _():
            spread(h, 0, c).start()

    def gather_in(h, root, c):
        @pl.when(c < first_tail)
        def _():
            tot[...] = gw_ref[rows_of(c), lanes_of(h)].astype(jnp.float32)

        @pl.when(c >= first_tail)
        def _():
            tot[...] = tail[rows_of(c - first_tail), lanes_of(h)].astype(jnp.float32)

        @pl.when(low & (z <= root))
        def _():
            chain(h, 0, c).wait_recv()
            tot[...] += rbuf[h, 0, rows_of(c)].astype(jnp.float32)

        @pl.when(high & (z >= root))
        def _():
            chain(h, 1, c).wait_recv()
            tot[...] += rbuf[h, 1, rows_of(c)].astype(jnp.float32)

        @pl.when(z == root)
        def _():
            gw_out[rows_of(c), lanes_of(h)] = (tot[...] * scale).astype(jnp.bfloat16)
            send_out(h, c, root)

        @pl.when(z != root)
        def _():
            sbuf[h, rows_of(c)] = tot[...].astype(jnp.bfloat16)

        @pl.when(z < root)
        def _():
            chain(h, 0, c).start()

        @pl.when(z > root)
        def _():
            chain(h, 1, c).start()

    far = n // 2

    def step(s, _):
        for h in range(2):
            root = n // 2 - h
            away = jnp.where(z < root, root - z, z - root)
            c = s - SLACK * (far - away)

            @pl.when((c >= 0) & (c < count))
            def _():
                gather_in(h, root, c)

            late = s - SLACK * (far + away)

            @pl.when((late >= 0) & (late < count) & (z != root))
            def _():
                spread(h, 0, late).wait_recv()
                send_out(h, late, root)

        return 0

    lax.fori_loop(0, first_tail, step, 0)

    def wait_back(i, _):
        back_copy(i, peer(i)).wait_recv()
        return 0

    lax.fori_loop(1, n_mp, wait_back, 0)
    for d in range(n_mp):
        flatret[d * cap : (d + 1) * cap, :] = ret[d].astype(jnp.float32)
    start = first_tail * ROWS
    tail[...] = (
        gw_ref[start:nb, :].astype(jnp.float32)
        + mm(hot_ref[...], flatret[...].astype(jnp.bfloat16))
    ).astype(jnp.bfloat16)
    lax.fori_loop(first_tail, count + 2 * SLACK * far, step, 0)

    def finish(i, _):
        gi_copy(i, peer(i)).wait_recv()
        return 0

    lax.fori_loop(1, n_mp, finish, 0)
    total = gi_ref[me].astype(jnp.float32)
    gbuf[me] = jnp.zeros(gbuf.shape[1:], gbuf.dtype)
    for d in range(n_mp):
        total = total + gbuf[d].astype(jnp.float32)
    gi_out[...] = total.astype(jnp.bfloat16)

    def sent(i, _):
        back_copy(i, None).wait_send()
        gi_copy(i, None).wait_send()
        return 0

    lax.fori_loop(1, n_mp, sent, 0)

    def sent_z(c, _):
        for h in range(2):
            root = n // 2 - h

            @pl.when(z != root)
            def _():
                chain(h, 0, c).wait_send()

            @pl.when(low & (z <= root))
            def _():
                spread(h, 1, c).wait_send()

            @pl.when(high & (z >= root))
            def _():
                spread(h, 0, c).wait_send()

        return 0

    lax.fori_loop(0, count, sent_z, 0)


def reduce_call(gw, gi_parts, gw_in, hot_tail, scale, data_count):
    nb, flat = gw.shape
    n_mp, tok_count, feat = gi_parts.shape
    count, half = nb // ROWS, flat // 2
    cap = gw_in.shape[1]
    dma = pltpu.SemaphoreType.DMA
    vm = pl.BlockSpec(memory_space=pltpu.VMEM)
    return pl.pallas_call(
        functools.partial(reduce_kernel, scale),
        out_shape=(
            jax.ShapeDtypeStruct((nb, flat), jnp.bfloat16),
            jax.ShapeDtypeStruct((tok_count, feat), jnp.bfloat16),
        ),
        in_specs=[vm] * 4,
        out_specs=(vm,) * 2,
        scratch_shapes=[
            pltpu.VMEM((2, 2, nb, half), jnp.bfloat16),
            pltpu.VMEM((2, nb, half), jnp.bfloat16),
            pltpu.VMEM(gi_parts.shape, jnp.bfloat16),
            pltpu.VMEM(gw_in.shape, jnp.bfloat16),
            pltpu.VMEM((n_mp * cap, flat), jnp.float32),
            pltpu.VMEM((hot_tail.shape[0], flat), jnp.bfloat16),
            pltpu.VMEM((ROWS, half), jnp.float32),
            dma((2, count)), dma((2, 2, count)), dma((2, 2, count)), dma((2, count)),
            dma((n_mp,)), dma((n_mp,)), dma((n_mp,)), dma((n_mp,)),
        ],
        compiler_params=pltpu.CompilerParams(
            collective_id=0, has_side_effects=True, vmem_limit_bytes=48 * 1024 * 1024
        ),
        name="reduce",
    )(gw, gi_parts, gw_in, hot_tail)


def cell_of(row, col):
    return (row // GROUP) * (GROUP * GROUP) + col * GROUP + row % GROUP


def plan(block_rows, block_cols, col_blocks, model_count, my_index):
    nb = block_rows.shape[0]
    target = block_cols // col_blocks
    home = target == my_index
    entry = jnp.arange(nb)
    earlier = (entry[None, :] < entry[:, None]) & (target[None, :] == target[:, None])
    rank = jnp.sum(earlier.astype(jnp.int32), axis=1)
    slot = jnp.where(home, -1, target * CAP + rank)
    local_col = block_cols % col_blocks
    return home, slot, local_col


def per_device(tokens, weight_blocks, block_rows, block_cols, importance, cotangent):
    tok_count = tokens.shape[0]
    model_count = lax.axis_size("mp")
    data_count = lax.axis_size("dp")
    my_index = lax.axis_index("mp")
    col_blocks = cotangent.shape[1] // BLOCK
    slots = model_count * CAP
    flat = BLOCK * BLOCK
    grad_scale = 1.0 / math.sqrt(tok_count * data_count)
    gathered = lax.all_gather(tokens, "mp", axis=0)
    home, slot, local_col = plan(block_rows, block_cols, col_blocks, model_count, my_index)
    send_hot = (jnp.arange(slots)[:, None] == slot[None, :])
    hot16 = send_hot.astype(jnp.bfloat16)
    payload = jnp.dot(hot16, weight_blocks, preferred_element_type=jnp.float32).astype(jnp.bfloat16)
    used = jnp.sum(send_hot * (local_col + 1)[None, :], axis=1)
    rows = jnp.sum(send_hot * block_rows[None, :], axis=1)
    meta = jnp.stack([rows, used], axis=1).astype(jnp.bfloat16)
    meta = jnp.pad(meta, ((0, 0), (0, 126)))
    payload = jnp.concatenate([payload, meta], axis=1).reshape(model_count, CAP, flat + 128)
    arrived = lax.all_to_all(payload, "mp", split_axis=0, concat_axis=0, tiled=True)
    arrived = arrived.reshape(slots, flat + 128)
    w_in = arrived[:, :flat]
    row_in = arrived[:, flat].astype(jnp.int32)
    col_in = arrived[:, flat + 1].astype(jnp.int32) - 1
    cell = jnp.where(home, cell_of(block_rows, local_col), -1)
    cell_in = jnp.where(col_in >= 0, cell_of(row_in, col_in), -1)
    weighted = importance.astype(jnp.float32) / 64.0
    up = (cotangent.astype(jnp.float32) * weighted[:, None]).astype(jnp.bfloat16)
    projected, gi_parts, gw, gw_in = dense_call(gathered, up, weight_blocks, w_in, cell, cell_in)
    tail_rows = min(-(-slots // ROWS) * ROWS, block_rows.shape[0])
    hot_tail = hot16.T[block_rows.shape[0] - tail_rows :]
    grad_weight, grad_input = reduce_call(
        gw, gi_parts, gw_in.reshape(model_count, CAP, flat), hot_tail, grad_scale, data_count
    )
    return (projected, grad_input, grad_weight)


def solution(mesh):
    return jax.shard_map(
        per_device,
        mesh=mesh,
        in_specs=(P("dp", "mp"), P("mp", None), P("mp"), P("mp"), P("dp"), P("dp", "mp")),
        out_specs=(P("dp", "mp"), P("dp", "mp"), P("mp", None)),
        check_vma=False,
    )
```

```python
import functools
import math

import jax
import jax.numpy as jnp
from jax import lax
from jax.experimental import pallas as pl
from jax.experimental.pallas import tpu as pltpu
from jax.sharding import PartitionSpec as P

BLOCK = 64
CAP = 3
GROUP = 8


def mm(a, b, dims=((1,), (0,))):
    return lax.dot_general(a, b, (dims, ((), ())), preferred_element_type=jnp.float32)


def swap_halves(x, y):
    width = x.shape[1]
    low = (lax.broadcasted_iota(jnp.int32, x.shape, 1) % 128) < 64
    first = jnp.where(low, x, pltpu.roll(y, 64, 1))
    second = jnp.where(low, pltpu.roll(x, width - 64, 1), y)
    return first, second


def dense_kernel(tok_ref, up_ref, w_ref, win_ref, crow_ref, crow_in_ref, ccol_ref, ccol_in_ref,
                 proj_ref, gi_ref, gw_ref, gw_in_ref,
                 wc_ref, wd_ref, gc_ref, gd_ref, acc_ref):
    d_count, tok_count, feat = tok_ref.shape
    cols = up_ref.shape[1]
    col_blocks = cols // BLOCK
    span = GROUP * BLOCK
    per = span // feat
    chunks = d_count // per
    cells = GROUP * col_blocks
    flat = BLOCK * BLOCK
    pairs = col_blocks // 2
    quads = BLOCK // 2
    src = lax.broadcasted_iota(jnp.int32, (span, span), 0)
    dst = lax.broadcasted_iota(jnp.int32, (span, span), 1)
    perm = ((src % BLOCK) * GROUP + src // BLOCK == dst).astype(jnp.float32).astype(jnp.bfloat16)
    acc_ref[...] = jnp.zeros_like(acc_ref)

    def chunk(j, _):
        base = j * cells
        ids = lax.broadcasted_iota(jnp.int32, (cells, 1), 0) + base
        hot = (ids == crow_ref[...]).astype(jnp.float32).astype(jnp.bfloat16)
        hot_in = (ids == crow_in_ref[...]).astype(jnp.float32).astype(jnp.bfloat16)
        wc_ref[...] = mm(hot, w_ref[...]) + mm(hot_in, win_ref[...])
        for p in range(pairs):
            a = wc_ref[2 * GROUP * p : 2 * GROUP * p + GROUP, :]
            b = wc_ref[2 * GROUP * p + GROUP : 2 * GROUP * (p + 1), :]
            even, odd = swap_halves(a, b)
            for q in range(quads):
                both = jnp.concatenate(
                    [even[:, 128 * q : 128 * (q + 1)], odd[:, 128 * q : 128 * (q + 1)]], axis=0
                )
                wd_ref[2 * GROUP * q : 2 * GROUP * (q + 1), 128 * p : 128 * (p + 1)] = both.astype(
                    jnp.bfloat16
                )
        parts = [tok_ref[j * per + g] for g in range(per)]
        tok = parts[0] if per == 1 else jnp.concatenate(parts, axis=1)
        tok_p = mm(tok, perm).astype(jnp.bfloat16)
        tok_t = mm(perm, tok, ((0,), (1,))).astype(jnp.bfloat16)
        acc_ref[...] += mm(tok_p, wd_ref[...])
        gi_p = mm(up_ref[...], wd_ref[...], ((1,), (1,))).astype(jnp.bfloat16)
        gi = mm(gi_p, perm, ((1,), (1,))).astype(jnp.bfloat16)
        for g in range(per):
            gi_ref[j * per + g] = gi[:, g * feat : (g + 1) * feat]
        gd_ref[...] = mm(tok_t, up_ref[...])
        for p in range(pairs):
            for q in range(quads):
                x = gd_ref[2 * GROUP * q : 2 * GROUP * q + GROUP, 128 * p : 128 * (p + 1)]
                y = gd_ref[2 * GROUP * q + GROUP : 2 * GROUP * (q + 1), 128 * p : 128 * (p + 1)]
                a, b = swap_halves(x, y)
                gc_ref[
                    pl.ds(pl.multiple_of(base + 2 * GROUP * p, 2 * GROUP), 2 * GROUP),
                    128 * q : 128 * (q + 1),
                ] = jnp.concatenate([a, b], axis=0).astype(jnp.bfloat16)
        return 0

    lax.fori_loop(0, chunks, chunk, 0)
    proj_ref[...] = acc_ref[...].astype(jnp.bfloat16)
    lanes = lax.broadcasted_iota(jnp.int32, (1, chunks * cells), 1)
    pick = (ccol_ref[...] == lanes).astype(jnp.float32).astype(jnp.bfloat16)
    pick_in = (ccol_in_ref[...] == lanes).astype(jnp.float32).astype(jnp.bfloat16)
    step = 512
    for s in range(flat // step):
        part = gc_ref[:, s * step : (s + 1) * step]
        gw_ref[:, s * step : (s + 1) * step] = mm(pick, part).astype(jnp.bfloat16)
        gw_in_ref[:, s * step : (s + 1) * step] = mm(pick_in, part).astype(jnp.bfloat16)


def dense_call(tok_all, up, weights, w_in, cell, cell_in):
    d_count, tok_count, feat = tok_all.shape
    cols = up.shape[1]
    span = GROUP * BLOCK
    cells = GROUP * (cols // BLOCK)
    chunks = d_count * feat // span
    flat = BLOCK * BLOCK
    nb, ns = weights.shape[0], w_in.shape[0]
    vm = pl.BlockSpec(memory_space=pltpu.VMEM)
    return pl.pallas_call(
        dense_kernel,
        out_shape=(
            jax.ShapeDtypeStruct((tok_count, cols), jnp.bfloat16),
            jax.ShapeDtypeStruct((d_count, tok_count, feat), jnp.bfloat16),
            jax.ShapeDtypeStruct((nb, flat), jnp.bfloat16),
            jax.ShapeDtypeStruct((ns, flat), jnp.bfloat16),
        ),
        in_specs=[vm] * 8,
        out_specs=(vm,) * 4,
        scratch_shapes=[
            pltpu.VMEM((cells, flat), jnp.float32),
            pltpu.VMEM((span, cols), jnp.bfloat16),
            pltpu.VMEM((chunks * cells, flat), jnp.bfloat16),
            pltpu.VMEM((span, cols), jnp.float32),
            pltpu.VMEM((tok_count, cols), jnp.float32),
        ],
        compiler_params=pltpu.CompilerParams(vmem_limit_bytes=48 * 1024 * 1024),
        name="dense",
    )(tok_all, up, weights, w_in, cell[None, :], cell_in[None, :], cell[:, None], cell_in[:, None])


MESH = pl.DeviceIdType.MESH
ROWS = 16
SLACK = 2


def reduce_kernel(scale, gw_ref, gi_ref, gin_ref, hot_ref, gw_out, gi_out,
                  rbuf, sbuf, gbuf, ret, flatret, tail, tot,
                  r_send, r_recv, b_send, b_recv, g_send, g_recv, q_send, q_recv):
    me, z = lax.axis_index("mp"), lax.axis_index("dp")
    n_mp, n = lax.axis_size("mp"), lax.axis_size("dp")
    nb, flat = gw_ref.shape
    half = flat // 2
    count = nb // ROWS
    tail_rows = tail.shape[0]
    cap = gin_ref.shape[1]
    first_tail = count - tail_rows // ROWS
    low, high = z > 0, z < n - 1

    barrier = pltpu.get_barrier_semaphore()

    def peer(i):
        return lax.rem(me + i, n_mp)

    def greet(i, _):
        pl.semaphore_signal(barrier, inc=1, device_id={"mp": peer(i)}, device_id_type=MESH)
        return 0

    lax.fori_loop(1, n_mp, greet, 0)

    @pl.when(low)
    def _():
        pl.semaphore_signal(barrier, inc=1, device_id={"dp": z - 1}, device_id_type=MESH)

    @pl.when(high)
    def _():
        pl.semaphore_signal(barrier, inc=1, device_id={"dp": z + 1}, device_id_type=MESH)

    pl.semaphore_wait(barrier, n_mp - 1 + low.astype(jnp.int32) + high.astype(jnp.int32))

    def back_copy(i, into):
        d = peer(i)
        return pltpu.make_async_remote_copy(
            src_ref=gin_ref.at[d], dst_ref=ret.at[me if into is None else into],
            send_sem=q_send.at[d], recv_sem=q_recv.at[me if into is None else into],
            device_id={"mp": d}, device_id_type=MESH)

    def gi_copy(i, into):
        d = peer(i)
        return pltpu.make_async_remote_copy(
            src_ref=gi_ref.at[d], dst_ref=gbuf.at[me if into is None else into],
            send_sem=g_send.at[d], recv_sem=g_recv.at[me if into is None else into],
            device_id={"mp": d}, device_id_type=MESH)

    def start_back(i, _):
        back_copy(i, None).start()
        return 0

    def start_gi(i, _):
        gi_copy(i, None).start()
        return 0

    lax.fori_loop(1, n_mp, start_back, 0)
    lax.fori_loop(1, n_mp, start_gi, 0)
    ret[me] = jnp.zeros(ret.shape[1:], ret.dtype)

    def rows_of(c):
        return pl.ds(pl.multiple_of(c * ROWS, ROWS), ROWS)

    def lanes_of(h):
        return slice(h * half, (h + 1) * half)

    def chain(h, side, c):
        target = z + 1 if side == 0 else z - 1
        return pltpu.make_async_remote_copy(
            src_ref=sbuf.at[h, rows_of(c)], dst_ref=rbuf.at[h, side, rows_of(c)],
            send_sem=r_send.at[h, c], recv_sem=r_recv.at[h, side, c],
            device_id={"dp": target}, device_id_type=MESH)

    def spread(h, side, c):
        target = z + 1 if side == 0 else z - 1
        return pltpu.make_async_remote_copy(
            src_ref=gw_out.at[rows_of(c), lanes_of(h)], dst_ref=gw_out.at[rows_of(c), lanes_of(h)],
            send_sem=b_send.at[h, side, c], recv_sem=b_recv.at[h, c],
            device_id={"dp": target}, device_id_type=MESH)

    def send_out(h, c, root):
        @pl.when(low & (z <= root))
        def _():
            spread(h, 1, c).start()

        @pl.when(high & (z >= root))
        def _():
            spread(h, 0, c).start()

    def gather_in(h, root, c):
        @pl.when(c < first_tail)
        def _():
            tot[...] = gw_ref[rows_of(c), lanes_of(h)].astype(jnp.float32)

        @pl.when(c >= first_tail)
        def _():
            tot[...] = tail[rows_of(c - first_tail), lanes_of(h)].astype(jnp.float32)

        @pl.when(low & (z <= root))
        def _():
            chain(h, 0, c).wait_recv()
            tot[...] += rbuf[h, 0, rows_of(c)].astype(jnp.float32)

        @pl.when(high & (z >= root))
        def _():
            chain(h, 1, c).wait_recv()
            tot[...] += rbuf[h, 1, rows_of(c)].astype(jnp.float32)

        @pl.when(z == root)
        def _():
            gw_out[rows_of(c), lanes_of(h)] = (tot[...] * scale).astype(jnp.bfloat16)
            send_out(h, c, root)

        @pl.when(z != root)
        def _():
            sbuf[h, rows_of(c)] = tot[...].astype(jnp.bfloat16)

        @pl.when(z < root)
        def _():
            chain(h, 0, c).start()

        @pl.when(z > root)
        def _():
            chain(h, 1, c).start()

    far = n // 2

    def step(s, _):
        for h in range(2):
            root = n // 2 - h
            away = jnp.where(z < root, root - z, z - root)
            c = s - SLACK * (far - away)

            @pl.when((c >= 0) & (c < count))
            def _():
                gather_in(h, root, c)

            late = s - SLACK * (far + away)

            @pl.when((late >= 0) & (late < count) & (z != root))
            def _():
                spread(h, 0, late).wait_recv()
                send_out(h, late, root)

        return 0

    lax.fori_loop(0, first_tail, step, 0)

    def wait_back(i, _):
        back_copy(i, peer(i)).wait_recv()
        return 0

    lax.fori_loop(1, n_mp, wait_back, 0)
    for d in range(n_mp):
        flatret[d * cap : (d + 1) * cap, :] = ret[d].astype(jnp.float32)
    start = first_tail * ROWS
    tail[...] = (
        gw_ref[start:nb, :].astype(jnp.float32)
        + mm(hot_ref[...], flatret[...].astype(jnp.bfloat16))
    ).astype(jnp.bfloat16)
    lax.fori_loop(first_tail, count + 2 * SLACK * far, step, 0)

    def finish(i, _):
        gi_copy(i, peer(i)).wait_recv()
        return 0

    lax.fori_loop(1, n_mp, finish, 0)
    total = gi_ref[me].astype(jnp.float32)
    gbuf[me] = jnp.zeros(gbuf.shape[1:], gbuf.dtype)
    for d in range(n_mp):
        total = total + gbuf[d].astype(jnp.float32)
    gi_out[...] = total.astype(jnp.bfloat16)

    def sent(i, _):
        back_copy(i, None).wait_send()
        gi_copy(i, None).wait_send()
        return 0

    lax.fori_loop(1, n_mp, sent, 0)

    def sent_z(c, _):
        for h in range(2):
            root = n // 2 - h

            @pl.when(z != root)
            def _():
                chain(h, 0, c).wait_send()

            @pl.when(low & (z <= root))
            def _():
                spread(h, 1, c).wait_send()

            @pl.when(high & (z >= root))
            def _():
                spread(h, 0, c).wait_send()

        return 0

    lax.fori_loop(0, count, sent_z, 0)


def reduce_call(gw, gi_parts, gw_in, hot_tail, scale, data_count):
    nb, flat = gw.shape
    n_mp, tok_count, feat = gi_parts.shape
    count, half = nb // ROWS, flat // 2
    cap = gw_in.shape[1]
    dma = pltpu.SemaphoreType.DMA
    vm = pl.BlockSpec(memory_space=pltpu.VMEM)
    return pl.pallas_call(
        functools.partial(reduce_kernel, scale),
        out_shape=(
            jax.ShapeDtypeStruct((nb, flat), jnp.bfloat16),
            jax.ShapeDtypeStruct((tok_count, feat), jnp.bfloat16),
        ),
        in_specs=[vm] * 4,
        out_specs=(vm,) * 2,
        scratch_shapes=[
            pltpu.VMEM((2, 2, nb, half), jnp.bfloat16),
            pltpu.VMEM((2, nb, half), jnp.bfloat16),
            pltpu.VMEM(gi_parts.shape, jnp.bfloat16),
            pltpu.VMEM(gw_in.shape, jnp.bfloat16),
            pltpu.VMEM((n_mp * cap, flat), jnp.float32),
            pltpu.VMEM((hot_tail.shape[0], flat), jnp.bfloat16),
            pltpu.VMEM((ROWS, half), jnp.float32),
            dma((2, count)), dma((2, 2, count)), dma((2, 2, count)), dma((2, count)),
            dma((n_mp,)), dma((n_mp,)), dma((n_mp,)), dma((n_mp,)),
        ],
        compiler_params=pltpu.CompilerParams(
            collective_id=0, has_side_effects=True, vmem_limit_bytes=48 * 1024 * 1024
        ),
        name="reduce",
    )(gw, gi_parts, gw_in, hot_tail)


def gather_kernel(tok_ref, pay_ref, tok_out, pay_out, t_send, t_recv, p_send, p_recv):
    me, n_mp = lax.axis_index("mp"), lax.axis_size("mp")
    barrier = pltpu.get_barrier_semaphore()

    def peer(i):
        return lax.rem(me + i, n_mp)

    def copies(i, slot):
        d = peer(i)
        return (
            pltpu.make_async_remote_copy(
                src_ref=pay_ref.at[d], dst_ref=pay_out.at[slot],
                send_sem=p_send.at[d], recv_sem=p_recv.at[slot],
                device_id={"mp": d}, device_id_type=MESH),
            pltpu.make_async_remote_copy(
                src_ref=tok_ref, dst_ref=tok_out.at[slot],
                send_sem=t_send.at[d], recv_sem=t_recv.at[slot],
                device_id={"mp": d}, device_id_type=MESH),
        )

    def greet(i, _):
        pl.semaphore_signal(barrier, inc=1, device_id={"mp": peer(i)}, device_id_type=MESH)
        return 0

    def start(i, _):
        for copy in copies(i, me):
            copy.start()
        return 0

    def arrive(i, _):
        for copy in copies(i, peer(i)):
            copy.wait_recv()
        return 0

    def leave(i, _):
        for copy in copies(i, me):
            copy.wait_send()
        return 0

    lax.fori_loop(1, n_mp, greet, 0)
    pl.semaphore_wait(barrier, n_mp - 1)
    lax.fori_loop(1, n_mp, start, 0)
    tok_out[me] = tok_ref[...]
    pay_out[me] = pay_ref[me]
    lax.fori_loop(1, n_mp, arrive, 0)
    lax.fori_loop(1, n_mp, leave, 0)


def gather_call(tokens, payload):
    n_mp = payload.shape[0]
    dma = pltpu.SemaphoreType.DMA
    vm = pl.BlockSpec(memory_space=pltpu.VMEM)
    return pl.pallas_call(
        gather_kernel,
        out_shape=(
            jax.ShapeDtypeStruct((n_mp,) + tokens.shape, jnp.bfloat16),
            jax.ShapeDtypeStruct(payload.shape, jnp.bfloat16),
        ),
        in_specs=[vm] * 2,
        out_specs=(vm,) * 2,
        scratch_shapes=[dma((n_mp,))] * 4,
        compiler_params=pltpu.CompilerParams(
            collective_id=1, has_side_effects=True, vmem_limit_bytes=32 * 1024 * 1024
        ),
        name="gather",
    )(tokens, payload)


def cell_of(row, col):
    return (row // GROUP) * (GROUP * GROUP) + col * GROUP + row % GROUP


def plan(block_rows, block_cols, col_blocks, model_count, my_index):
    nb = block_rows.shape[0]
    target = block_cols // col_blocks
    home = target == my_index
    entry = jnp.arange(nb)
    earlier = (entry[None, :] < entry[:, None]) & (target[None, :] == target[:, None])
    rank = jnp.sum(earlier.astype(jnp.int32), axis=1)
    slot = jnp.where(home, -1, target * CAP + rank)
    local_col = block_cols % col_blocks
    return home, slot, local_col


def per_device(tokens, weight_blocks, block_rows, block_cols, importance, cotangent):
    tok_count = tokens.shape[0]
    model_count = lax.axis_size("mp")
    data_count = lax.axis_size("dp")
    my_index = lax.axis_index("mp")
    col_blocks = cotangent.shape[1] // BLOCK
    slots = model_count * CAP
    flat = BLOCK * BLOCK
    grad_scale = 1.0 / math.sqrt(tok_count * data_count)
    home, slot, local_col = plan(block_rows, block_cols, col_blocks, model_count, my_index)
    send_hot = (jnp.arange(slots)[:, None] == slot[None, :])
    hot16 = send_hot.astype(jnp.bfloat16)
    payload = jnp.dot(hot16, weight_blocks, preferred_element_type=jnp.float32).astype(jnp.bfloat16)
    used = jnp.sum(send_hot * (local_col + 1)[None, :], axis=1)
    rows = jnp.sum(send_hot * block_rows[None, :], axis=1)
    meta = jnp.stack([rows, used], axis=1).astype(jnp.bfloat16)
    meta = jnp.pad(meta, ((0, 0), (0, 126)))
    payload = jnp.concatenate([payload, meta], axis=1).reshape(model_count, CAP, flat + 128)
    gathered, arrived = gather_call(tokens, payload)
    arrived = arrived.reshape(slots, flat + 128)
    w_in = arrived[:, :flat]
    row_in = arrived[:, flat].astype(jnp.int32)
    col_in = arrived[:, flat + 1].astype(jnp.int32) - 1
    cell = jnp.where(home, cell_of(block_rows, local_col), -1)
    cell_in = jnp.where(col_in >= 0, cell_of(row_in, col_in), -1)
    weighted = importance.astype(jnp.float32) / 64.0
    up = (cotangent.astype(jnp.float32) * weighted[:, None]).astype(jnp.bfloat16)
    projected, gi_parts, gw, gw_in = dense_call(gathered, up, weight_blocks, w_in, cell, cell_in)
    tail_rows = min(-(-slots // ROWS) * ROWS, block_rows.shape[0])
    hot_tail = hot16.T[block_rows.shape[0] - tail_rows :]
    grad_weight, grad_input = reduce_call(
        gw, gi_parts, gw_in.reshape(model_count, CAP, flat), hot_tail, grad_scale, data_count
    )
    return (projected, grad_input, grad_weight)


def solution(mesh):
    return jax.shard_map(
        per_device,
        mesh=mesh,
        in_specs=(P("dp", "mp"), P("mp", None), P("mp"), P("mp"), P("dp"), P("dp", "mp")),
        out_specs=(P("dp", "mp"), P("dp", "mp"), P("mp", None)),
        check_vma=False,
    )
```

```python
import functools
import math

import jax
import jax.numpy as jnp
from jax import lax
from jax.experimental import pallas as pl
from jax.experimental.pallas import tpu as pltpu
from jax.sharding import PartitionSpec as P

BLOCK = 64
CAP = 3
GROUP = 8


def mm(a, b, dims=((1,), (0,))):
    return lax.dot_general(a, b, (dims, ((), ())), preferred_element_type=jnp.float32)


def swap_halves(x, y):
    width = x.shape[1]
    low = (lax.broadcasted_iota(jnp.int32, x.shape, 1) % 128) < 64
    first = jnp.where(low, x, pltpu.roll(y, 64, 1))
    second = jnp.where(low, pltpu.roll(x, width - 64, 1), y)
    return first, second


def dense_kernel(tok_ref, up_ref, w_ref, win_ref, crow_ref, crow_in_ref, ccol_ref, ccol_in_ref,
                 proj_ref, gi_ref, gw_ref, gw_in_ref,
                 wc_ref, wd_ref, gc_ref, gd_ref, acc_ref):
    d_count, tok_count, feat = tok_ref.shape
    cols = up_ref.shape[1]
    col_blocks = cols // BLOCK
    span = GROUP * BLOCK
    per = span // feat
    chunks = d_count // per
    cells = GROUP * col_blocks
    flat = BLOCK * BLOCK
    pairs = col_blocks // 2
    quads = BLOCK // 2
    src = lax.broadcasted_iota(jnp.int32, (span, span), 0)
    dst = lax.broadcasted_iota(jnp.int32, (span, span), 1)
    perm = ((src % BLOCK) * GROUP + src // BLOCK == dst).astype(jnp.float32).astype(jnp.bfloat16)
    acc_ref[...] = jnp.zeros_like(acc_ref)

    def chunk(j, _):
        base = j * cells
        ids = lax.broadcasted_iota(jnp.int32, (cells, 1), 0) + base
        hot = (ids == crow_ref[...]).astype(jnp.float32).astype(jnp.bfloat16)
        hot_in = (ids == crow_in_ref[...]).astype(jnp.float32).astype(jnp.bfloat16)
        wc_ref[...] = mm(hot, w_ref[...]) + mm(hot_in, win_ref[...])
        for p in range(pairs):
            a = wc_ref[2 * GROUP * p : 2 * GROUP * p + GROUP, :]
            b = wc_ref[2 * GROUP * p + GROUP : 2 * GROUP * (p + 1), :]
            even, odd = swap_halves(a, b)
            for q in range(quads):
                both = jnp.concatenate(
                    [even[:, 128 * q : 128 * (q + 1)], odd[:, 128 * q : 128 * (q + 1)]], axis=0
                )
                wd_ref[2 * GROUP * q : 2 * GROUP * (q + 1), 128 * p : 128 * (p + 1)] = both.astype(
                    jnp.bfloat16
                )
        parts = [tok_ref[j * per + g] for g in range(per)]
        tok = parts[0] if per == 1 else jnp.concatenate(parts, axis=1)
        tok_p = mm(tok, perm).astype(jnp.bfloat16)
        tok_t = mm(perm, tok, ((0,), (1,))).astype(jnp.bfloat16)
        acc_ref[...] += mm(tok_p, wd_ref[...])
        gi_p = mm(up_ref[...], wd_ref[...], ((1,), (1,))).astype(jnp.bfloat16)
        gi = mm(gi_p, perm, ((1,), (1,))).astype(jnp.bfloat16)
        for g in range(per):
            gi_ref[j * per + g] = gi[:, g * feat : (g + 1) * feat]
        gd_ref[...] = mm(tok_t, up_ref[...])
        for p in range(pairs):
            for q in range(quads):
                x = gd_ref[2 * GROUP * q : 2 * GROUP * q + GROUP, 128 * p : 128 * (p + 1)]
                y = gd_ref[2 * GROUP * q + GROUP : 2 * GROUP * (q + 1), 128 * p : 128 * (p + 1)]
                a, b = swap_halves(x, y)
                gc_ref[
                    pl.ds(pl.multiple_of(base + 2 * GROUP * p, 2 * GROUP), 2 * GROUP),
                    128 * q : 128 * (q + 1),
                ] = jnp.concatenate([a, b], axis=0).astype(jnp.bfloat16)
        return 0

    lax.fori_loop(0, chunks, chunk, 0)
    proj_ref[...] = acc_ref[...].astype(jnp.bfloat16)
    lanes = lax.broadcasted_iota(jnp.int32, (1, chunks * cells), 1)
    pick = (ccol_ref[...] == lanes).astype(jnp.float32).astype(jnp.bfloat16)
    pick_in = (ccol_in_ref[...] == lanes).astype(jnp.float32).astype(jnp.bfloat16)
    step = 512
    for s in range(flat // step):
        part = gc_ref[:, s * step : (s + 1) * step]
        gw_ref[:, s * step : (s + 1) * step] = mm(pick, part).astype(jnp.bfloat16)
        gw_in_ref[:, s * step : (s + 1) * step] = mm(pick_in, part).astype(jnp.bfloat16)


def dense_call(tok_all, up, weights, w_in, cell, cell_in):
    d_count, tok_count, feat = tok_all.shape
    cols = up.shape[1]
    span = GROUP * BLOCK
    cells = GROUP * (cols // BLOCK)
    chunks = d_count * feat // span
    flat = BLOCK * BLOCK
    nb, ns = weights.shape[0], w_in.shape[0]
    vm = pl.BlockSpec(memory_space=pltpu.VMEM)
    return pl.pallas_call(
        dense_kernel,
        out_shape=(
            jax.ShapeDtypeStruct((tok_count, cols), jnp.bfloat16),
            jax.ShapeDtypeStruct((d_count, tok_count, feat), jnp.bfloat16),
            jax.ShapeDtypeStruct((nb, flat), jnp.bfloat16),
            jax.ShapeDtypeStruct((ns, flat), jnp.bfloat16),
        ),
        in_specs=[vm] * 8,
        out_specs=(vm,) * 4,
        scratch_shapes=[
            pltpu.VMEM((cells, flat), jnp.float32),
            pltpu.VMEM((span, cols), jnp.bfloat16),
            pltpu.VMEM((chunks * cells, flat), jnp.bfloat16),
            pltpu.VMEM((span, cols), jnp.float32),
            pltpu.VMEM((tok_count, cols), jnp.float32),
        ],
        compiler_params=pltpu.CompilerParams(vmem_limit_bytes=48 * 1024 * 1024),
        name="dense",
    )(tok_all, up, weights, w_in, cell[None, :], cell_in[None, :], cell[:, None], cell_in[:, None])


MESH = pl.DeviceIdType.MESH
ROWS = 16
SLACK = 2


def reduce_kernel(scale, gw_ref, gi_ref, gin_ref, hot_ref, gw_out, gi_out,
                  rbuf, sbuf, gbuf, ret, flatret, tail, tot,
                  r_send, r_recv, b_send, b_recv, g_send, g_recv, q_send, q_recv):
    me, z = lax.axis_index("mp"), lax.axis_index("dp")
    n_mp, n = lax.axis_size("mp"), lax.axis_size("dp")
    nb, flat = gw_ref.shape
    half = flat // 2
    count = nb // ROWS
    tail_rows = tail.shape[0]
    cap = gin_ref.shape[1]
    first_tail = count - tail_rows // ROWS
    low, high = z > 0, z < n - 1

    barrier = pltpu.get_barrier_semaphore()

    def peer(i):
        return lax.rem(me + i, n_mp)

    def greet(i, _):
        pl.semaphore_signal(barrier, inc=1, device_id={"mp": peer(i)}, device_id_type=MESH)
        return 0

    lax.fori_loop(1, n_mp, greet, 0)

    @pl.when(low)
    def _():
        pl.semaphore_signal(barrier, inc=1, device_id={"dp": z - 1}, device_id_type=MESH)

    @pl.when(high)
    def _():
        pl.semaphore_signal(barrier, inc=1, device_id={"dp": z + 1}, device_id_type=MESH)

    pl.semaphore_wait(barrier, n_mp - 1 + low.astype(jnp.int32) + high.astype(jnp.int32))

    def back_copy(i, into):
        d = peer(i)
        return pltpu.make_async_remote_copy(
            src_ref=gin_ref.at[d], dst_ref=ret.at[me if into is None else into],
            send_sem=q_send.at[d], recv_sem=q_recv.at[me if into is None else into],
            device_id={"mp": d}, device_id_type=MESH)

    def gi_copy(i, into):
        d = peer(i)
        return pltpu.make_async_remote_copy(
            src_ref=gi_ref.at[d], dst_ref=gbuf.at[me if into is None else into],
            send_sem=g_send.at[d], recv_sem=g_recv.at[me if into is None else into],
            device_id={"mp": d}, device_id_type=MESH)

    def start_back(i, _):
        back_copy(i, None).start()
        return 0

    def start_gi(i, _):
        gi_copy(i, None).start()
        return 0

    lax.fori_loop(1, n_mp, start_back, 0)
    lax.fori_loop(1, n_mp, start_gi, 0)
    ret[me] = jnp.zeros(ret.shape[1:], ret.dtype)

    def rows_of(c):
        return pl.ds(pl.multiple_of(c * ROWS, ROWS), ROWS)

    def lanes_of(h):
        return slice(h * half, (h + 1) * half)

    def chain(h, side, c):
        target = z + 1 if side == 0 else z - 1
        return pltpu.make_async_remote_copy(
            src_ref=sbuf.at[h, rows_of(c)], dst_ref=rbuf.at[h, side, rows_of(c)],
            send_sem=r_send.at[h, c], recv_sem=r_recv.at[h, side, c],
            device_id={"dp": target}, device_id_type=MESH)

    def spread(h, side, c):
        target = z + 1 if side == 0 else z - 1
        return pltpu.make_async_remote_copy(
            src_ref=gw_out.at[rows_of(c), lanes_of(h)], dst_ref=gw_out.at[rows_of(c), lanes_of(h)],
            send_sem=b_send.at[h, side, c], recv_sem=b_recv.at[h, c],
            device_id={"dp": target}, device_id_type=MESH)

    def send_out(h, c, root):
        @pl.when(low & (z <= root))
        def _():
            spread(h, 1, c).start()

        @pl.when(high & (z >= root))
        def _():
            spread(h, 0, c).start()

    def gather_in(h, root, c):
        @pl.when(c < first_tail)
        def _():
            tot[...] = gw_ref[rows_of(c), lanes_of(h)].astype(jnp.float32)

        @pl.when(c >= first_tail)
        def _():
            tot[...] = tail[rows_of(c - first_tail), lanes_of(h)].astype(jnp.float32)

        @pl.when(low & (z <= root))
        def _():
            chain(h, 0, c).wait_recv()
            tot[...] += rbuf[h, 0, rows_of(c)].astype(jnp.float32)

        @pl.when(high & (z >= root))
        def _():
            chain(h, 1, c).wait_recv()
            tot[...] += rbuf[h, 1, rows_of(c)].astype(jnp.float32)

        @pl.when(z == root)
        def _():
            gw_out[rows_of(c), lanes_of(h)] = (tot[...] * scale).astype(jnp.bfloat16)
            send_out(h, c, root)

        @pl.when(z != root)
        def _():
            sbuf[h, rows_of(c)] = tot[...].astype(jnp.bfloat16)

        @pl.when(z < root)
        def _():
            chain(h, 0, c).start()

        @pl.when(z > root)
        def _():
            chain(h, 1, c).start()

    far = n // 2

    def step(s, _):
        for h in range(2):
            root = n // 2 - h
            away = jnp.where(z < root, root - z, z - root)
            c = s - SLACK * (far - away)

            @pl.when((c >= 0) & (c < count))
            def _():
                gather_in(h, root, c)

            late = s - SLACK * (far + away)

            @pl.when((late >= 0) & (late < count) & (z != root))
            def _():
                spread(h, 0, late).wait_recv()
                send_out(h, late, root)

        return 0

    lax.fori_loop(0, first_tail, step, 0)

    def wait_back(i, _):
        back_copy(i, peer(i)).wait_recv()
        return 0

    lax.fori_loop(1, n_mp, wait_back, 0)
    for d in range(n_mp):
        flatret[d * cap : (d + 1) * cap, :] = ret[d].astype(jnp.float32)
    start = first_tail * ROWS
    tail[...] = (
        gw_ref[start:nb, :].astype(jnp.float32)
        + mm(hot_ref[...], flatret[...].astype(jnp.bfloat16))
    ).astype(jnp.bfloat16)
    lax.fori_loop(first_tail, count + 2 * SLACK * far, step, 0)

    def finish(i, _):
        gi_copy(i, peer(i)).wait_recv()
        return 0

    lax.fori_loop(1, n_mp, finish, 0)
    total = gi_ref[me].astype(jnp.float32)
    gbuf[me] = jnp.zeros(gbuf.shape[1:], gbuf.dtype)
    for d in range(n_mp):
        total = total + gbuf[d].astype(jnp.float32)
    gi_out[...] = total.astype(jnp.bfloat16)

    def sent(i, _):
        back_copy(i, None).wait_send()
        gi_copy(i, None).wait_send()
        return 0

    lax.fori_loop(1, n_mp, sent, 0)

    def sent_z(c, _):
        for h in range(2):
            root = n // 2 - h

            @pl.when(z != root)
            def _():
                chain(h, 0, c).wait_send()

            @pl.when(low & (z <= root))
            def _():
                spread(h, 1, c).wait_send()

            @pl.when(high & (z >= root))
            def _():
                spread(h, 0, c).wait_send()

        return 0

    lax.fori_loop(0, count, sent_z, 0)


def reduce_call(gw, gi_parts, gw_in, hot_tail, scale, data_count):
    nb, flat = gw.shape
    n_mp, tok_count, feat = gi_parts.shape
    count, half = nb // ROWS, flat // 2
    cap = gw_in.shape[1]
    dma = pltpu.SemaphoreType.DMA
    vm = pl.BlockSpec(memory_space=pltpu.VMEM)
    return pl.pallas_call(
        functools.partial(reduce_kernel, scale),
        out_shape=(
            jax.ShapeDtypeStruct((nb, flat), jnp.bfloat16),
            jax.ShapeDtypeStruct((tok_count, feat), jnp.bfloat16),
        ),
        in_specs=[vm] * 4,
        out_specs=(vm,) * 2,
        scratch_shapes=[
            pltpu.VMEM((2, 2, nb, half), jnp.bfloat16),
            pltpu.VMEM((2, nb, half), jnp.bfloat16),
            pltpu.VMEM(gi_parts.shape, jnp.bfloat16),
            pltpu.VMEM(gw_in.shape, jnp.bfloat16),
            pltpu.VMEM((n_mp * cap, flat), jnp.float32),
            pltpu.VMEM((hot_tail.shape[0], flat), jnp.bfloat16),
            pltpu.VMEM((ROWS, half), jnp.float32),
            dma((2, count)), dma((2, 2, count)), dma((2, 2, count)), dma((2, count)),
            dma((n_mp,)), dma((n_mp,)), dma((n_mp,)), dma((n_mp,)),
        ],
        compiler_params=pltpu.CompilerParams(
            collective_id=0, has_side_effects=True, vmem_limit_bytes=48 * 1024 * 1024
        ),
        name="reduce",
    )(gw, gi_parts, gw_in, hot_tail)


def gather_kernel(tok_ref, pay_ref, tok_out, pay_out, t_send, t_recv, p_send, p_recv):
    me, n_mp = lax.axis_index("mp"), lax.axis_size("mp")
    barrier = pltpu.get_barrier_semaphore()

    def peer(i):
        return lax.rem(me + i, n_mp)

    def twin(i):
        return i + 1 - 2 * lax.rem(i, 2)

    def pay(i, slot):
        d = peer(i)
        return pltpu.make_async_remote_copy(
            src_ref=pay_ref.at[d], dst_ref=pay_out.at[slot],
            send_sem=p_send.at[d], recv_sem=p_recv.at[slot],
            device_id={"mp": d}, device_id_type=MESH)

    def far(q, slot):
        d = peer(2 * q)
        return pltpu.make_async_remote_copy(
            src_ref=tok_ref, dst_ref=tok_out.at[slot],
            send_sem=t_send.at[d], recv_sem=t_recv.at[slot],
            device_id={"mp": d}, device_id_type=MESH)

    def near(src, sent, slot):
        return pltpu.make_async_remote_copy(
            src_ref=src, dst_ref=tok_out.at[slot],
            send_sem=t_send.at[twin(sent)], recv_sem=t_recv.at[slot],
            device_id={"mp": twin(me)}, device_id_type=MESH)

    def greet(i, _):
        pl.semaphore_signal(barrier, inc=1, device_id={"mp": peer(i)}, device_id_type=MESH)
        return 0

    def start_pay(i, _):
        pay(i, me).start()
        return 0

    def start_far(q, _):
        far(q, me).start()
        return 0

    def hand_on(q, _):
        d = peer(2 * q)
        far(q, d).wait_recv()
        near(tok_out.at[d], d, d).start()
        return 0

    def arrive(q, _):
        near(tok_ref, me, twin(peer(2 * q))).wait_recv()
        return 0

    def finish(i, _):
        pay(i, peer(i)).wait_recv()
        pay(i, me).wait_send()
        return 0

    def leave(q, _):
        far(q, me).wait_send()
        near(tok_out.at[peer(2 * q)], peer(2 * q), peer(2 * q)).wait_send()
        return 0

    lax.fori_loop(1, n_mp, greet, 0)
    pl.semaphore_wait(barrier, n_mp - 1)
    lax.fori_loop(1, n_mp, start_pay, 0)
    lax.fori_loop(1, n_mp // 2, start_far, 0)
    near(tok_ref, me, me).start()
    tok_out[me] = tok_ref[...]
    pay_out[me] = pay_ref[me]
    lax.fori_loop(1, n_mp // 2, hand_on, 0)
    lax.fori_loop(0, n_mp // 2, arrive, 0)
    lax.fori_loop(1, n_mp, finish, 0)
    lax.fori_loop(1, n_mp // 2, leave, 0)
    near(tok_ref, me, me).wait_send()


def gather_call(tokens, payload):
    n_mp = payload.shape[0]
    dma = pltpu.SemaphoreType.DMA
    vm = pl.BlockSpec(memory_space=pltpu.VMEM)
    return pl.pallas_call(
        gather_kernel,
        out_shape=(
            jax.ShapeDtypeStruct((n_mp,) + tokens.shape, jnp.bfloat16),
            jax.ShapeDtypeStruct(payload.shape, jnp.bfloat16),
        ),
        in_specs=[vm] * 2,
        out_specs=(vm,) * 2,
        scratch_shapes=[dma((n_mp,))] * 4,
        compiler_params=pltpu.CompilerParams(
            collective_id=1, has_side_effects=True, vmem_limit_bytes=32 * 1024 * 1024
        ),
        name="gather",
    )(tokens, payload)


def cell_of(row, col):
    return (row // GROUP) * (GROUP * GROUP) + col * GROUP + row % GROUP


def plan(block_rows, block_cols, col_blocks, model_count, my_index):
    nb = block_rows.shape[0]
    target = block_cols // col_blocks
    home = target == my_index
    entry = jnp.arange(nb)
    earlier = (entry[None, :] < entry[:, None]) & (target[None, :] == target[:, None])
    rank = jnp.sum(earlier.astype(jnp.int32), axis=1)
    slot = jnp.where(home, -1, target * CAP + rank)
    local_col = block_cols % col_blocks
    return home, slot, local_col


def per_device(tokens, weight_blocks, block_rows, block_cols, importance, cotangent):
    tok_count = tokens.shape[0]
    model_count = lax.axis_size("mp")
    data_count = lax.axis_size("dp")
    my_index = lax.axis_index("mp")
    col_blocks = cotangent.shape[1] // BLOCK
    slots = model_count * CAP
    flat = BLOCK * BLOCK
    grad_scale = 1.0 / math.sqrt(tok_count * data_count)
    home, slot, local_col = plan(block_rows, block_cols, col_blocks, model_count, my_index)
    send_hot = (jnp.arange(slots)[:, None] == slot[None, :])
    hot16 = send_hot.astype(jnp.bfloat16)
    payload = jnp.dot(hot16, weight_blocks, preferred_element_type=jnp.float32).astype(jnp.bfloat16)
    used = jnp.sum(send_hot * (local_col + 1)[None, :], axis=1)
    rows = jnp.sum(send_hot * block_rows[None, :], axis=1)
    meta = jnp.stack([rows, used], axis=1).astype(jnp.bfloat16)
    meta = jnp.pad(meta, ((0, 0), (0, 126)))
    payload = jnp.concatenate([payload, meta], axis=1).reshape(model_count, CAP, flat + 128)
    gathered, arrived = gather_call(tokens, payload)
    arrived = arrived.reshape(slots, flat + 128)
    w_in = arrived[:, :flat]
    row_in = arrived[:, flat].astype(jnp.int32)
    col_in = arrived[:, flat + 1].astype(jnp.int32) - 1
    cell = jnp.where(home, cell_of(block_rows, local_col), -1)
    cell_in = jnp.where(col_in >= 0, cell_of(row_in, col_in), -1)
    weighted = importance.astype(jnp.float32) / 64.0
    up = (cotangent.astype(jnp.float32) * weighted[:, None]).astype(jnp.bfloat16)
    projected, gi_parts, gw, gw_in = dense_call(gathered, up, weight_blocks, w_in, cell, cell_in)
    tail_rows = min(-(-slots // ROWS) * ROWS, block_rows.shape[0])
    hot_tail = hot16.T[block_rows.shape[0] - tail_rows :]
    grad_weight, grad_input = reduce_call(
        gw, gi_parts, gw_in.reshape(model_count, CAP, flat), hot_tail, grad_scale, data_count
    )
    return (projected, grad_input, grad_weight)


def solution(mesh):
    return jax.shard_map(
        per_device,
        mesh=mesh,
        in_specs=(P("dp", "mp"), P("mp", None), P("mp"), P("mp"), P("dp"), P("dp", "mp")),
        out_specs=(P("dp", "mp"), P("dp", "mp"), P("mp", None)),
        check_vma=False,
    )
```
